512 devices in a mesh: seq: 32 (over x, z_lo, core), exp: 16 (over z_hi, y).
Axes of the slice: x: 4, y: 4, z: 16 (z_hi: 4, z_lo: 4; z = z_hi * 4 + z_lo), core: 2. Of those that a mesh axis runs over, the one named last changes fastest.
Arguments:
- tokens: bfloat16 [2, 16384, 1024], P(None, 'seq'), may hold values from -48 to 48
- router: bfloat16 [1024, 2048], P(None, 'exp'), may hold values from -4 to 4
- w_in: bfloat16 [512, 1024, 512], P(('exp', 'seq')), may hold values from -0.1875 to 0.1875
- w_out: bfloat16 [512, 512, 1024], P(('exp', 'seq')), may hold values from -0.125 to 0.125
Outputs:
- mixed: bfloat16 [2, 16384, 1024], P(None, ('seq', 'exp'))
The draws below stay inside these ranges and needn't reach their ends.
All inputs are finite; a program needn't handle non-finite values.
Results may differ from the reference program's by a relative error of at most 0.015.
Values may be sent and summed in bfloat16 or wider, within the bound.
No kernel may reach another device: no remote copies, remote signals or barrier semaphores. Data moves between devices by JAX's collectives and lax.ppermute only.
A program may use at most 64 MiB of HBM per device.

```python
import jax
import jax.numpy as jnp
from jax import lax

D = 1024
FF = 2048
EXP_DEV = 8
SLOTS = 16
SEQS = 2
EXPERTS = 128
LEN = 16384
FF_SPLIT = 4
N_SEQ = 32


def draw_tokens(key, part):
    noise_key = jax.random.fold_in(jax.random.fold_in(key, 1), 0)
    base_noise = jnp.clip(jax.random.normal(noise_key, (SEQS, LEN, D), jnp.float32), -6.0, 6.0)
    position = jnp.arange(LEN, dtype=jnp.float32) / max(LEN - 1, 1)
    ramp_scale = 0.85 + 0.5 * position
    values = base_noise * ramp_scale[None, :, None]
    return values.astype(jnp.bfloat16)


def draw_router(key, part):
    noise_key = jax.random.fold_in(jax.random.fold_in(key, 2), 0)
    base_noise = jnp.clip(jax.random.normal(noise_key, (D, EXPERTS * SLOTS), jnp.float32), -6.0, 6.0)
    values = base_noise * (2.0 / D) ** 0.5
    return values.astype(jnp.bfloat16)


def level_of(stream_key, extent, pieces, smallest, high):
    gain = 1.0
    for axis_at, shards_of in pieces:
        heights = jax.random.uniform(jax.random.fold_in(jax.random.fold_in(stream_key, 6), axis_at), (shards_of,), jnp.float32, smallest / len(pieces), high / len(pieces))
        gain = gain * jnp.repeat(jnp.exp(heights), extent[axis_at] // shards_of).reshape((-1,) + (1,) * (len(extent) - 1 - axis_at))
    return gain


def centred(own_key, extent, spread, bound, pieces=(), kind=jnp.bfloat16):
    array = jax.random.normal(own_key, extent, jnp.float32) * spread
    if len(pieces) > 0:
        array = level_of(own_key, extent, pieces, -0.22, 0.18) * array
    return jnp.clip(array, min=-bound, max=bound).astype(kind)


def setup_inputs(seed: int = 0) -> dict:
    seeds = jax.random.split(jax.random.key(seed), 5)
    return {
        "tokens": draw_tokens(jax.random.fold_in(seeds[4], 71), 0),
        "router": draw_router(jax.random.fold_in(seeds[4], 71), 0),
        "w_in": centred(seeds[2], (EXPERTS * FF_SPLIT, D, FF // FF_SPLIT), D ** -0.5, 0.1875, ((0, 512),)),
        "w_out": centred(seeds[3], (EXPERTS * FF_SPLIT, FF // FF_SPLIT, D), FF ** -0.5, 0.125, ((0, 512),)),
    }


def reference(tokens, router, w_in, w_out):
    router_logits = jnp.einsum("bnq,qt->bnt", tokens.astype(jnp.float32), router.astype(jnp.float32))
    dispatch_weights = jax.nn.softmax(router_logits, axis=1).astype(jnp.bfloat16)
    slot_input_rows = jnp.einsum("mja,mjo->mao", dispatch_weights.astype(jnp.float32), tokens.astype(jnp.float32)).astype(jnp.bfloat16)
    split_count = N_SEQ // EXP_DEV
    piece_width = FF // split_count
    first_stack = w_in.reshape(EXPERTS, split_count, D, piece_width)
    second_stack = w_out.reshape(EXPERTS, split_count, piece_width, D)
    grouped_inputs = slot_input_rows.reshape(SEQS, EXPERTS, SLOTS, D)

    def apply_expert_network(expert_index):
        first_full = jnp.transpose(first_stack[expert_index], (1, 0, 2)).reshape(D, FF)
        second_full = second_stack[expert_index].reshape(FF, D)
        expert_input = grouped_inputs[:, expert_index].reshape(SEQS * SLOTS, D)
        pre_active = jnp.dot(expert_input, first_full, preferred_element_type=jnp.float32)
        hidden = jax.nn.gelu(pre_active, approximate=True).astype(jnp.bfloat16)
        result = jnp.dot(hidden, second_full, preferred_element_type=jnp.float32).astype(jnp.bfloat16)
        return result.reshape(SEQS, SLOTS, D)

    per_expert = lax.map(apply_expert_network, jnp.arange(EXPERTS, dtype=jnp.int32))
    slot_output_rows = jnp.transpose(per_expert, (1, 0, 2, 3)).reshape(SEQS, EXPERTS * SLOTS, D)
    combine_weights = jax.nn.softmax(router_logits, axis=2).astype(jnp.bfloat16)
    mixed = jnp.einsum("ptx,pxg->ptg", combine_weights.astype(jnp.float32), slot_output_rows.astype(jnp.float32))
    return mixed.astype(jnp.bfloat16)
```

```python
import jax
import jax.numpy as jnp
from jax import lax
from jax.sharding import Mesh
from jax.sharding import PartitionSpec as P

SLOTS = 16
AXES = ("x", "zla", "zlb", "c", "zh", "y")
SEQ = ("x", "zla", "zlb", "c")
EXP = ("zh", "y")
f32, bf16 = jnp.float32, jnp.bfloat16


def swap(tiles, axis):
    return lax.all_to_all(tiles, axis, split_axis=0, concat_axis=0, tiled=True)


def in_three(v):
    hi = lax.reduce_precision(v, 8, 7)
    mid = lax.reduce_precision(v - hi, 8, 7)
    return [hi, mid, v - hi - mid]


def columns(parts, width=128):
    both = jnp.concatenate(parts, axis=-1)
    spare = [(0, 0)] * (both.ndim - 1) + [(0, width - both.shape[-1])]
    return jnp.pad(both, spare).astype(bf16)


def whole(cols):
    cols = cols.astype(f32)
    top = cols[..., 0:1] + cols[..., 1:2] + cols[..., 2:3]
    total = cols[..., 3:4] + cols[..., 4:5] + cols[..., 5:6]
    return top, total


def blend(rows, axis):
    width = rows.shape[-1] - 128
    top, total = whole(rows[..., width:])
    share = total * jnp.exp(top - top.max(axis=axis, keepdims=True))
    share = share / share.sum(axis=axis, keepdims=True)
    return (rows[..., :width].astype(f32) * share).sum(axis=axis).astype(bf16)


def shards(tokens, router, w_in, w_out):
    slots = router.shape[1]
    experts = slots // SLOTS
    width = tokens.shape[2]
    each = tokens.shape[1]
    nx, nzla, nzlb, nc, nzh, ny = (lax.axis_size(a) for a in AXES)
    chunk = each // nzh

    with jax.named_scope("tokens_c"):
        own = swap(tokens, "c")
        flat = own.reshape(nc * each, width)
        pair = [(0, 1), (1, 0)]
        w_in2 = lax.ppermute(w_in, "c", pair)
        w_out2 = lax.ppermute(w_out, "c", pair)

    with jax.named_scope("logits"):
        logits = jnp.einsum("dn,td->nt", router, flat, preferred_element_type=f32)
        top = logits.max(axis=1, keepdims=True)
        e1 = jnp.exp(logits - top)
        total = e1.sum(axis=1, keepdims=True)
        part = jnp.dot(e1.astype(bf16), flat, preferred_element_type=f32) / total
        stats = columns(in_three(top) + in_three(total))
        send = jnp.concatenate([part.astype(bf16), stats], axis=1)
        send = send.reshape(nx * nzla, 1, SLOTS, width + 128)
        send = jnp.broadcast_to(send, (nx * nzla, nzlb, SLOTS, width + 128))
        send = send.reshape(-1, SLOTS, width + 128)

    with jax.named_scope("slots_xzl"):
        arrived = swap(send, ("x", "zla", "zlb"))

    with jax.named_scope("ffn"):
        rows = blend(arrived, 0)
        out = 0.0
        for a, b in ((w_in, w_out), (w_in2, w_out2)):
            hidden = jnp.dot(rows, a[0], preferred_element_type=f32)
            hidden = jax.nn.gelu(hidden, approximate=True).astype(bf16)
            out = out + jnp.dot(hidden, b[0], preferred_element_type=f32)
        out = out.astype(bf16)

    with jax.named_scope("out_zl"):
        got = swap(jnp.broadcast_to(out, (nzla * nzlb, *out.shape)), ("zla", "zlb"))
        got = got.reshape(nzla, nzlb, SLOTS, width).astype(f32).sum(axis=1).astype(bf16)

    with jax.named_scope("row_exp"):
        m2 = logits.max(axis=0, keepdims=True)
        e2 = jnp.exp(logits - m2).astype(bf16)
        e2 = e2.reshape(slots, nc, nzh, chunk).transpose(2, 1, 0, 3)
        m2 = jnp.concatenate(in_three(m2), axis=0).reshape(3, nc, nzh, chunk)
        m2 = jnp.pad(m2.transpose(2, 1, 0, 3), ((0, 0), (0, 0), (0, 5), (0, 0)))
        row = jnp.concatenate(
            [
                e2.reshape(nzh, nc * slots, chunk),
                m2.astype(bf16).reshape(nzh, nc * 8, chunk),
                jnp.broadcast_to(got.reshape(1, -1, chunk), (nzh, got.size // chunk, chunk)),
            ],
            axis=1,
        )

    with jax.named_scope("out_zh"):
        row = swap(row, "zh")

    with jax.named_scope("out_x"):
        at = nc * slots + nc * 8
        found = row[:, at:].reshape(nzh, nzla * SLOTS, width)
        found = swap(jnp.broadcast_to(found, (nx, *found.shape)), "x")

    with jax.named_scope("mix"):
        e2 = row[:, : nc * slots].reshape(nzh, nc, slots, chunk).astype(f32)
        m2 = row[:, nc * slots : at].reshape(nzh, nc, 8, chunk).astype(f32)
        m2 = m2[:, :, 0] + m2[:, :, 1] + m2[:, :, 2]
        top = m2.max(axis=0)
        e2 = e2 * jnp.exp(m2 - top)[:, :, None, :]
        total = e2.sum(axis=(0, 2))
        mix = (e2 / total[None, :, None, :]).astype(bf16)
        mix = mix.reshape(nzh, nc, nx, nzla * SLOTS, chunk)
        out = jnp.einsum("zcxrt,xzrg->ctg", mix, found, preferred_element_type=f32)
        stats = columns([s[:, :, None] for s in in_three(top) + in_three(total)])
        out = jnp.concatenate([out.astype(bf16), stats], axis=2)
        out = out.reshape(nc * ny, chunk // ny, width + 128)

    with jax.named_scope("out_cy"):
        out = swap(out, ("c", "y")).reshape(nc, ny, chunk // ny, width + 128)

    with jax.named_scope("last"):
        return blend(out, 1)


def solution(mesh):
    torus = Mesh(mesh.devices.reshape(4, 2, 2, 2, 4, 4), AXES)
    placed = (P(None, SEQ, None), P(None, EXP), P(EXP + SEQ, None, None), P(EXP + SEQ, None, None))
    return jax.shard_map(
        shards, mesh=torus, in_specs=placed, out_specs=P(None, SEQ + EXP, None), check_vma=False
    )
```

```python
import functools

import jax
import jax.numpy as jnp
from jax import lax
from jax.experimental import pallas as pl
from jax.experimental.pallas import tpu as pltpu
from jax.sharding import Mesh
from jax.sharding import PartitionSpec as P

SLOTS = 16
LANES = 128
AXES = ("x", "zla", "zlb", "c", "zh", "y")
SEQ = ("x", "zla", "zlb", "c")
EXP = ("zh", "y")
f32, bf16 = jnp.float32, jnp.bfloat16


def swap(tiles, axis):
    return lax.all_to_all(tiles, axis, split_axis=0, concat_axis=0, tiled=True)


def in_three(v):
    hi = v.astype(bf16).astype(f32)
    mid = (v - hi).astype(bf16).astype(f32)
    return [hi, mid, v - hi - mid]


def as_columns(parts):
    lane = lax.broadcasted_iota(jnp.int32, (parts[0].shape[0], LANES), 1)
    out = jnp.zeros(lane.shape, f32)
    for k, part in enumerate(parts):
        out = jnp.where(lane == k, part, out)
    return out.astype(bf16)


def blend(ref, pieces):
    width = ref.shape[-1] - LANES
    tops, totals = [], []
    for k in pieces:
        cols = ref[(*k, slice(None), slice(width, width + LANES))].astype(f32)
        tops.append(cols[:, 0:1] + cols[:, 1:2] + cols[:, 2:3])
        totals.append(cols[:, 3:4] + cols[:, 4:5] + cols[:, 5:6])
    top = functools.reduce(jnp.maximum, tops)
    shares = [s * jnp.exp(t - top) for t, s in zip(tops, totals)]
    scale = 1.0 / functools.reduce(jnp.add, shares)
    out = 0.0
    for k, share in zip(pieces, shares):
        out = out + ref[(*k, slice(None), slice(0, width))].astype(f32) * (share * scale)
    return out


def score_kernel(tok_ref, router_ref, send_ref, logit_ref):
    tok = tok_ref[...].reshape(-1, tok_ref.shape[-1])
    width = tok.shape[1]
    logits = jnp.dot(tok, router_ref[...], preferred_element_type=f32)
    logit_ref[...] = logits
    logits = logits.T
    top = logits.max(axis=1, keepdims=True)
    e1 = jnp.exp(logits - top)
    total = e1.sum(axis=1, keepdims=True)
    part = jnp.dot(e1.astype(bf16), tok, preferred_element_type=f32) * (1.0 / total)
    part = part.astype(bf16)
    stats = as_columns(in_three(top) + in_three(total))
    experts = logits.shape[0] // SLOTS
    copies = send_ref.shape[0] // experts
    for e in range(experts):
        for k in range(copies):
            send_ref[e * copies + k, :, 0:width] = part[e * SLOTS : (e + 1) * SLOTS]
            send_ref[e * copies + k, :, width:] = stats[e * SLOTS : (e + 1) * SLOTS]


def row_kernel(at_ref, logit_ref, *refs):
    outs, hold = refs[:-1], refs[-1]
    n, slots = len(outs), logit_ref.shape[1]
    cores = logit_ref.shape[0] // (n * LANES)
    per = LANES // n
    zero = jnp.zeros((1, LANES), f32)
    for y in range(n):
        rows = []
        for c in range(cores):
            at = [(c * n + z) * LANES + y * per for z in range(n)]
            logits = jnp.concatenate([logit_ref[i : i + per] for i in at], axis=0).T
            top = logits.max(axis=0, keepdims=True)
            hold[y, c * slots : (c + 1) * slots] = jnp.exp(logits - top).astype(bf16)
            rows += in_three(top) + [zero] * 5
        hold[y, cores * slots :] = jnp.concatenate(rows, axis=0).astype(bf16)
    for k in range(n):
        outs[k][...] = hold[(at_ref[0] + k) % n]


def ffn_kernel(got_ref, a_ref, a2_ref, b_ref, b2_ref, out_ref):
    rows = blend(got_ref, [(k,) for k in range(got_ref.shape[0])]).astype(bf16)
    out = 0.0
    for a, b in ((a_ref, b_ref), (a2_ref, b2_ref)):
        hidden = jnp.dot(rows, a[0], preferred_element_type=f32)
        hidden = jax.nn.gelu(hidden, approximate=True).astype(bf16)
        out = out + jnp.dot(hidden, b[0], preferred_element_type=f32)
    out = out.astype(bf16)
    for k in range(out_ref.shape[0]):
        out_ref[k] = out


def mix_kernel(at_ref, r0, r1, r2, r3, found_ref, out_ref):
    rs = (r0, r1, r2, r3)
    n, slots = len(rs), found_ref.shape[0] * found_ref.shape[2]
    width = found_ref.shape[-1]
    cores = r0.shape[0] // slots
    nz = out_ref.shape[0] // cores
    per = LANES // nz
    weights, stats = [[] for _ in rs], []
    for c in range(cores):
        tops = []
        for r in rs:
            m = r[cores * slots :].astype(f32)[8 * c : 8 * c + 8]
            tops.append(m[0:1] + m[1:2] + m[2:3])
        top = functools.reduce(jnp.maximum, tops)
        e2 = [
            r[c * slots : (c + 1) * slots].astype(f32) * jnp.exp(t - top)
            for r, t in zip(rs, tops)
        ]
        total = functools.reduce(jnp.add, [e.sum(axis=0, keepdims=True) for e in e2])
        scale = 1.0 / total
        for k in range(n):
            weights[k].append((e2[k] * scale).T.astype(bf16))
        zero = jnp.zeros((2, LANES), f32)
        rows = jnp.concatenate(in_three(top) + in_three(total) + [zero], axis=0)
        stats.append(rows.astype(bf16))
    out = 0.0
    for k in range(n):
        y = (at_ref[0] + n - k) % n
        block = found_ref[:, y].reshape(slots, width)
        out = out + jnp.dot(jnp.concatenate(weights[k], axis=0), block, preferred_element_type=f32)
    out = out.astype(bf16)
    for c in range(cores):
        for z in range(nz):
            at, to = c * LANES + z * per, c * nz + z
            for j in range(width // LANES):
                out_ref[to, j * per : (j + 1) * per] = out[at : at + per, j * LANES : (j + 1) * LANES]
            out_ref[to, width // LANES * per :] = stats[c]


def last_kernel(at_ref, got_ref, out_ref, hold):
    seqs, per, width = out_ref.shape
    n = got_ref.shape[0] // seqs
    end = width // LANES * per
    both = [got_ref[k, end:].astype(f32) for k in range(seqs * n)]
    both = both + [jnp.zeros((LANES - 8 * len(both), LANES), f32)]
    hold[...] = jnp.concatenate(both, axis=0).T
    cols = hold[pl.ds(at_ref[0] * per, per)]
    for s in range(seqs):
        tops, totals = [], []
        for k in range(n):
            i = 8 * (s * n + k)
            tops.append(cols[:, i : i + 1] + cols[:, i + 1 : i + 2] + cols[:, i + 2 : i + 3])
            totals.append(cols[:, i + 3 : i + 4] + cols[:, i + 4 : i + 5] + cols[:, i + 5 : i + 6])
        top = functools.reduce(jnp.maximum, tops)
        shares = [d * jnp.exp(t - top) for t, d in zip(tops, totals)]
        scale = 1.0 / functools.reduce(jnp.add, shares)
        shares = [v * scale for v in shares]
        for j in range(width // LANES):
            out = 0.0
            for k in range(n):
                out = out + got_ref[s * n + k, j * per : (j + 1) * per].astype(f32) * shares[k]
            out_ref[s, :, j * LANES : (j + 1) * LANES] = out.astype(bf16)


def call(kernel, outs, *args, scalar=False, scratch=()):
    kind = pltpu.MemorySpace.VMEM
    specs = [pl.BlockSpec(memory_space=kind) for _ in args]
    if scalar:
        specs[0] = pl.BlockSpec(memory_space=pltpu.MemorySpace.SMEM)
    return pl.pallas_call(
        kernel,
        out_shape=outs,
        in_specs=specs,
        out_specs=jax.tree.map(lambda _: pl.BlockSpec(memory_space=kind), outs),
        scratch_shapes=scratch,
        compiler_params=pltpu.CompilerParams(vmem_limit_bytes=40 << 20),
    )(*args)


def shape(*lengths, kind=bf16):
    return jax.ShapeDtypeStruct(lengths, kind)


def shards(tokens, router, w_in, w_out):
    slots = router.shape[1]
    width = tokens.shape[2]
    each = tokens.shape[1]
    nx, nzla, nzlb, nc, nzh, ny = (lax.axis_size(a) for a in AXES)
    assert each == nzh * LANES and slots == nx * nzla * SLOTS
    assert nzh == ny == nx
    here_y = lax.axis_index("y").astype(jnp.int32).reshape(1)
    here_zh = lax.axis_index("zh").astype(jnp.int32).reshape(1)
    per = LANES // nzh

    own = swap(tokens, "c")

    send, logits = call(
        score_kernel,
        (shape(nx * nzla * nzlb, SLOTS, width + LANES), shape(nc * each, slots, kind=f32)),
        own,
        router,
    )

    arrived = swap(send, ("x", "zla", "zlb"))

    pair = [(0, 1), (1, 0)]
    w_in2 = lax.ppermute(w_in, "c", pair)
    w_out2 = lax.ppermute(w_out, "c", pair)

    block = nc * (slots + 8)
    rows = call(
        row_kernel,
        (shape(block, LANES),) * ny,
        here_y,
        logits,
        scalar=True,
        scratch=(pltpu.VMEM((ny, block, LANES), bf16),),
    )

    rows = list(rows)
    for k in range(1, ny):
        rows[k] = lax.ppermute(rows[k], "y", [(i, (i + k) % ny) for i in range(ny)])

    out = call(ffn_kernel, shape(nzla * nzlb, SLOTS, width), arrived, w_in, w_in2, w_out, w_out2)

    got = swap(out, ("zla", "zlb"))
    got = got.reshape(nzla, nzlb, SLOTS, width).astype(f32).sum(axis=1).astype(bf16)
    got = got.reshape(nzla * SLOTS, width)

    found = swap(jnp.broadcast_to(got, (nx * ny, *got.shape)), ("x", "y"))
    found = found.reshape(nx, ny, *got.shape)

    block = width // LANES * per + 8
    out = call(mix_kernel, shape(nc * nzh, block, LANES), here_y, *rows, found, scalar=True)

    out = swap(out, ("c", "zh"))

    return call(
        last_kernel,
        shape(nc, per, width),
        here_zh,
        out,
        scalar=True,
        scratch=(pltpu.VMEM((LANES, LANES), f32),),
    )


def solution(mesh):
    torus = Mesh(mesh.devices.reshape(4, 2, 2, 2, 4, 4), AXES)
    placed = (P(None, SEQ, None), P(None, EXP), P(EXP + SEQ, None, None), P(EXP + SEQ, None, None))
    return jax.shard_map(
        shards, mesh=torus, in_specs=placed, out_specs=P(None, SEQ + EXP, None), check_vma=False
    )
```

```python
import functools

import jax
import jax.numpy as jnp
from jax import lax
from jax.experimental import pallas as pl
from jax.experimental.pallas import tpu as pltpu
from jax.sharding import Mesh
from jax.sharding import PartitionSpec as P

SLOTS = 16
LANES = 128
AXES = ("x", "zla", "zlb", "c", "zh", "y")
SEQ = ("x", "zla", "zlb", "c")
EXP = ("zh", "y")
f32, bf16 = jnp.float32, jnp.bfloat16


def swap(tiles, axis):
    return lax.all_to_all(tiles, axis, split_axis=0, concat_axis=0, tiled=True)


def in_three(v):
    hi = v.astype(bf16).astype(f32)
    mid = (v - hi).astype(bf16).astype(f32)
    return [hi, mid, v - hi - mid]


def as_columns(parts):
    lane = lax.broadcasted_iota(jnp.int32, (parts[0].shape[0], LANES), 1)
    out = jnp.zeros(lane.shape, f32)
    for k, part in enumerate(parts):
        out = jnp.where(lane == k, part, out)
    return out.astype(bf16)


def blend(ref, pieces):
    width = ref.shape[-1] - LANES
    tops, totals = [], []
    for k in pieces:
        cols = ref[(*k, slice(None), slice(width, width + LANES))].astype(f32)
        tops.append(cols[:, 0:1] + cols[:, 1:2] + cols[:, 2:3])
        totals.append(cols[:, 3:4] + cols[:, 4:5] + cols[:, 5:6])
    top = functools.reduce(jnp.maximum, tops)
    shares = [s * jnp.exp(t - top) for t, s in zip(tops, totals)]
    scale = 1.0 / functools.reduce(jnp.add, shares)
    out = 0.0
    for k, share in zip(pieces, shares):
        out = out + ref[(*k, slice(None), slice(0, width))].astype(f32) * (share * scale)
    return out


def score_kernel(tok_ref, router_ref, send_ref, logit_ref):
    tok = tok_ref[...].reshape(-1, tok_ref.shape[-1])
    width = tok.shape[1]
    logits = jnp.dot(tok, router_ref[...], preferred_element_type=f32)
    logit_ref[...] = logits
    logits = logits.T
    top = logits.max(axis=1, keepdims=True)
    e1 = jnp.exp(logits - top)
    total = e1.sum(axis=1, keepdims=True)
    part = jnp.dot(e1.astype(bf16), tok, preferred_element_type=f32) * (1.0 / total)
    part = part.astype(bf16)
    stats = as_columns(in_three(top) + in_three(total))
    experts = logits.shape[0] // SLOTS
    copies = send_ref.shape[0] // experts
    for e in range(experts):
        for k in range(copies):
            send_ref[e * copies + k, :, 0:width] = part[e * SLOTS : (e + 1) * SLOTS]
            send_ref[e * copies + k, :, width:] = stats[e * SLOTS : (e + 1) * SLOTS]


def row_kernel(at_ref, logit_ref, *refs):
    outs, hold = refs[:-1], refs[-1]
    n, slots = len(outs), logit_ref.shape[1]
    cores = logit_ref.shape[0] // (n * LANES)
    per = LANES // n
    zero = jnp.zeros((1, LANES), f32)
    for y in range(n):
        rows = []
        for c in range(cores):
            at = [(c * n + (at_ref[1] + j) % n) * LANES + y * per for j in range(n)]
            at = [pl.multiple_of(i, per) for i in at]
            logits = jnp.concatenate([logit_ref[pl.ds(i, per)] for i in at], axis=0).T
            top = logits.max(axis=0, keepdims=True)
            hold[y, c * slots : (c + 1) * slots] = jnp.exp(logits - top).astype(bf16)
            rows += in_three(top) + [zero] * 5
        hold[y, cores * slots :] = jnp.concatenate(rows, axis=0).astype(bf16)
    for k in range(n):
        outs[k][...] = hold[(at_ref[0] + k) % n]


def ffn_kernel(got_ref, a_ref, a2_ref, b_ref, b2_ref, out_ref):
    rows = blend(got_ref, [(k,) for k in range(got_ref.shape[0])]).astype(bf16)
    out = 0.0
    for a, b in ((a_ref, b_ref), (a2_ref, b2_ref)):
        hidden = jnp.dot(rows, a[0], preferred_element_type=f32)
        hidden = jax.nn.gelu(hidden, approximate=True).astype(bf16)
        out = out + jnp.dot(hidden, b[0], preferred_element_type=f32)
    out = out.astype(bf16)
    for k in range(out_ref.shape[0]):
        out_ref[k] = out


def pair_kernel(got_ref, out_ref):
    pairs = out_ref.shape[1] // SLOTS
    each = got_ref.shape[0] // pairs
    for p in range(pairs):
        out = 0.0
        for k in range(each):
            out = out + got_ref[p * each + k].astype(f32)
        out = out.astype(bf16)
        for k in range(out_ref.shape[0]):
            out_ref[k, p * SLOTS : (p + 1) * SLOTS] = out


def mix_kernel(at_ref, r0, r1, r2, r3, found_ref, *outs):
    rs = (r0, r1, r2, r3)
    n, slots = len(rs), found_ref.shape[0] * found_ref.shape[2]
    width = found_ref.shape[-1]
    cores = r0.shape[0] // slots
    nz = len(outs)
    per = LANES // nz
    weights, stats = [[] for _ in rs], []
    for c in range(cores):
        tops = []
        for r in rs:
            m = r[cores * slots :].astype(f32)[8 * c : 8 * c + 8]
            tops.append(m[0:1] + m[1:2] + m[2:3])
        top = functools.reduce(jnp.maximum, tops)
        e2 = [
            r[c * slots : (c + 1) * slots].astype(f32) * jnp.exp(t - top)
            for r, t in zip(rs, tops)
        ]
        total = functools.reduce(jnp.add, [e.sum(axis=0, keepdims=True) for e in e2])
        scale = 1.0 / total
        for k in range(n):
            weights[k].append((e2[k] * scale).T.astype(bf16))
        zero = jnp.zeros((2, LANES), f32)
        rows = jnp.concatenate(in_three(top) + in_three(total) + [zero], axis=0)
        stats.append(rows)
    out = 0.0
    for k in range(n):
        y = (at_ref[0] + n - k) % n
        block = found_ref[:, y].reshape(slots, width)
        out = out + jnp.dot(jnp.concatenate(weights[k], axis=0), block, preferred_element_type=f32)
    out = out.astype(bf16)
    for c in range(cores):
        for z in range(nz):
            at = c * LANES + z * per
            for j in range(width // LANES):
                outs[z][c, j * per : (j + 1) * per] = out[at : at + per, j * LANES : (j + 1) * LANES]
            outs[z][c, width // LANES * per :] = stats[c].astype(bf16)


def last_kernel(at_ref, *refs):
    gots, (keep_ref, give_ref, hold) = refs[:-3], refs[-3:]
    cores, per, width = hold.shape
    n = len(gots)
    end = width // LANES * per
    both = [gots[k][c, end:].astype(f32) for c in range(cores) for k in range(n)]
    both = both + [jnp.zeros((LANES - 8 * len(both), LANES), f32)]
    both = jnp.concatenate(both, axis=0).T
    for c in range(cores):
        tops, totals = [], []
        for k in range(n):
            i, cols = 8 * (c * n + k), both[k * per : (k + 1) * per]
            tops.append(cols[:, i : i + 1] + cols[:, i + 1 : i + 2] + cols[:, i + 2 : i + 3])
            totals.append(cols[:, i + 3 : i + 4] + cols[:, i + 4 : i + 5] + cols[:, i + 5 : i + 6])
        top = functools.reduce(jnp.maximum, tops)
        shares = [d * jnp.exp(t - top) for t, d in zip(tops, totals)]
        scale = 1.0 / functools.reduce(jnp.add, shares)
        shares = [v * scale for v in shares]
        for j in range(width // LANES):
            out = 0.0
            for k in range(n):
                out = out + gots[k][c, j * per : (j + 1) * per].astype(f32) * shares[k]
            hold[c, :, j * LANES : (j + 1) * LANES] = out.astype(bf16)
    keep_ref[...] = hold[at_ref[2]]
    give_ref[...] = hold[1 - at_ref[2]]


def join_kernel(at_ref, keep_ref, got_ref, out_ref):
    out_ref[at_ref[2]] = keep_ref[...]
    out_ref[1 - at_ref[2]] = got_ref[1 - at_ref[2]]


def call(kernel, outs, *args, scalar=False, scratch=(), mib=16):
    kind = pltpu.MemorySpace.VMEM
    specs = [pl.BlockSpec(memory_space=kind) for _ in args]
    if scalar:
        specs[0] = pl.BlockSpec(memory_space=pltpu.MemorySpace.SMEM)
    return pl.pallas_call(
        kernel,
        out_shape=outs,
        in_specs=specs,
        out_specs=jax.tree.map(lambda _: pl.BlockSpec(memory_space=kind), outs),
        scratch_shapes=scratch,
        compiler_params=pltpu.CompilerParams(vmem_limit_bytes=mib << 20),
    )(*args)


def shape(*lengths, kind=bf16):
    return jax.ShapeDtypeStruct(lengths, kind)


def shards(tokens, router, w_in, w_out):
    slots = router.shape[1]
    width = tokens.shape[2]
    each = tokens.shape[1]
    nx, nzla, nzlb, nc, nzh, ny = (lax.axis_size(a) for a in AXES)
    assert each == nzh * LANES and slots == nx * nzla * SLOTS
    assert nzh == ny == nx
    here = jnp.stack([lax.axis_index(a).astype(jnp.int32) for a in ("y", "zh", "c")])
    per = LANES // nzh

    own = swap(tokens, "c")

    send, logits = call(
        score_kernel,
        (shape(nx * nzla * nzlb, SLOTS, width + LANES), shape(nc * each, slots, kind=f32)),
        own,
        router,
    )

    arrived = swap(send, ("x", "zla", "zlb"))

    pair = [(0, 1), (1, 0)]
    w_in2 = lax.ppermute(w_in, "c", pair)
    w_out2 = lax.ppermute(w_out, "c", pair)

    block = nc * (slots + 8)
    rows = call(
        row_kernel,
        (shape(block, LANES),) * ny,
        here,
        logits,
        scalar=True,
        scratch=(pltpu.VMEM((ny, block, LANES), bf16),),
    )

    rows = list(rows)
    for k in range(1, ny):
        rows[k] = lax.ppermute(rows[k], "y", [(i, (i + k) % ny) for i in range(ny)])

    out = call(ffn_kernel, shape(nzla * nzlb, SLOTS, width), arrived, w_in, w_in2, w_out, w_out2)

    got = swap(out, ("zla", "zlb"))

    got = call(pair_kernel, shape(nx * ny, nzla * SLOTS, width), got)

    found = swap(got, ("x", "y")).reshape(nx, ny, nzla * SLOTS, width)

    block = width // LANES * per + 8
    outs = list(call(mix_kernel, (shape(nc, block, LANES),) * nzh, here, *rows, found, scalar=True))

    for k in range(1, nzh):
        outs[k] = lax.ppermute(outs[k], "zh", [(i, (i + k) % nzh) for i in range(nzh)])

    keep, give = call(
        last_kernel,
        (shape(per, width),) * 2,
        here,
        *outs,
        scalar=True,
        scratch=(pltpu.VMEM((nc, per, width), bf16),),
    )

    got = lax.all_gather(give, "c")

    return call(join_kernel, shape(nc, per, width), here, keep, got, scalar=True)


def solution(mesh):
    torus = Mesh(mesh.devices.reshape(4, 2, 2, 2, 4, 4), AXES)
    placed = (P(None, SEQ, None), P(None, EXP), P(EXP + SEQ, None, None), P(EXP + SEQ, None, None))
    return jax.shard_map(
        shards, mesh=torus, in_specs=placed, out_specs=P(None, SEQ + EXP, None), check_vma=False
    )
```

```python
import functools

import jax
import jax.numpy as jnp
from jax import lax
from jax.experimental import pallas as pl
from jax.experimental.pallas import tpu as pltpu
from jax.sharding import Mesh
from jax.sharding import PartitionSpec as P

SLOTS = 16
LANES = 128
AXES = ("x", "zla", "zlb", "c", "zh", "y")
SEQ = ("x", "zla", "zlb", "c")
EXP = ("zh", "y")
f32, bf16 = jnp.float32, jnp.bfloat16


def swap(tiles, axis):
    return lax.all_to_all(tiles, axis, split_axis=0, concat_axis=0, tiled=True)


def in_three(v):
    hi = v.astype(bf16).astype(f32)
    mid = (v - hi).astype(bf16).astype(f32)
    return [hi, mid, v - hi - mid]


def as_columns(parts):
    lane = lax.broadcasted_iota(jnp.int32, (parts[0].shape[0], LANES), 1)
    out = jnp.zeros(lane.shape, f32)
    for k, part in enumerate(parts):
        out = jnp.where(lane == k, part, out)
    return out.astype(bf16)


def blend(ref, pieces):
    width = ref.shape[-1] - LANES
    tops, totals = [], []
    for k in pieces:
        cols = ref[(*k, slice(None), slice(width, width + LANES))].astype(f32)
        tops.append(cols[:, 0:1] + cols[:, 1:2] + cols[:, 2:3])
        totals.append(cols[:, 3:4] + cols[:, 4:5] + cols[:, 5:6])
    top = functools.reduce(jnp.maximum, tops)
    shares = [s * jnp.exp(t - top) for t, s in zip(tops, totals)]
    scale = 1.0 / functools.reduce(jnp.add, shares)
    out = 0.0
    for k, share in zip(pieces, shares):
        out = out + ref[(*k, slice(None), slice(0, width))].astype(f32) * (share * scale)
    return out


def score_kernel(tok_ref, router_ref, send_ref, logit_ref):
    tok = tok_ref[...].reshape(-1, tok_ref.shape[-1])
    width = tok.shape[1]
    logits = jnp.dot(tok, router_ref[...], preferred_element_type=f32)
    logit_ref[...] = logits
    logits = logits.T
    top = logits.max(axis=1, keepdims=True)
    e1 = jnp.exp(logits - top)
    total = e1.sum(axis=1, keepdims=True)
    part = jnp.dot(e1.astype(bf16), tok, preferred_element_type=f32) * (1.0 / total)
    part = part.astype(bf16)
    stats = as_columns(in_three(top) + in_three(total))
    experts = logits.shape[0] // SLOTS
    copies = send_ref.shape[0] // experts
    for e in range(experts):
        for k in range(copies):
            send_ref[e * copies + k, :, 0:width] = part[e * SLOTS : (e + 1) * SLOTS]
            send_ref[e * copies + k, :, width:] = stats[e * SLOTS : (e + 1) * SLOTS]


def row_kernel(at_ref, logit_ref, *refs):
    outs, hold = refs[:-1], refs[-1]
    n, slots = len(outs), logit_ref.shape[1]
    cores = logit_ref.shape[0] // (n * LANES)
    per = LANES // n
    zero = jnp.zeros((1, LANES), f32)
    for y in range(n):
        rows = []
        for c in range(cores):
            at = [((at_ref[2] ^ c) * n + (at_ref[1] ^ j)) * LANES + y * per for j in range(n)]
            at = [pl.multiple_of(i, per) for i in at]
            logits = jnp.concatenate([logit_ref[pl.ds(i, per)] for i in at], axis=0).T
            top = logits.max(axis=0, keepdims=True)
            hold[y, c * slots : (c + 1) * slots] = jnp.exp(logits - top).astype(bf16)
            rows += in_three(top) + [zero] * 5
        hold[y, cores * slots :] = jnp.concatenate(rows, axis=0).astype(bf16)
    for k in range(n):
        outs[k][...] = hold[at_ref[0] ^ k]


def ffn_kernel(got_ref, a_ref, b_ref, a2_hbm, b2_hbm, out_ref, a2_ref, b2_ref, sem):
    copies = (
        pltpu.make_async_copy(a2_hbm, a2_ref, sem.at[0]),
        pltpu.make_async_copy(b2_hbm, b2_ref, sem.at[1]),
    )
    for copy in copies:
        copy.start()
    rows = blend(got_ref, [(k,) for k in range(got_ref.shape[0])]).astype(bf16)

    def part(a, b):
        hidden = jnp.dot(rows, a[0], preferred_element_type=f32)
        hidden = jax.nn.gelu(hidden, approximate=True).astype(bf16)
        return jnp.dot(hidden, b[0], preferred_element_type=f32)

    out = part(a_ref, b_ref)
    for copy in copies:
        copy.wait()
    out = (out + part(a2_ref, b2_ref)).astype(bf16)
    for k in range(out_ref.shape[0]):
        out_ref[k] = out


def pair_kernel(got_ref, out_ref):
    pairs = out_ref.shape[1] // SLOTS
    each = got_ref.shape[0] // pairs
    for p in range(pairs):
        out = 0.0
        for k in range(each):
            out = out + got_ref[p * each + k].astype(f32)
        out = out.astype(bf16)
        for k in range(out_ref.shape[0]):
            out_ref[k, p * SLOTS : (p + 1) * SLOTS] = out


def mix_kernel(at_ref, r0, r1, r2, r3, found_ref, *outs):
    rs = (r0, r1, r2, r3)
    n, slots = len(rs), found_ref.shape[0] * found_ref.shape[2]
    width = found_ref.shape[-1]
    cores = r0.shape[0] // slots
    nz = len(outs)
    per = LANES // nz
    weights, stats = [[] for _ in rs], []
    for c in range(cores):
        tops = []
        for r in rs:
            m = r[cores * slots :].astype(f32)[8 * c : 8 * c + 8]
            tops.append(m[0:1] + m[1:2] + m[2:3])
        top = functools.reduce(jnp.maximum, tops)
        e2 = [
            r[c * slots : (c + 1) * slots].astype(f32) * jnp.exp(t - top)
            for r, t in zip(rs, tops)
        ]
        total = functools.reduce(jnp.add, [e.sum(axis=0, keepdims=True) for e in e2])
        scale = 1.0 / total
        for k in range(n):
            weights[k].append((e2[k] * scale).T.astype(bf16))
        zero = jnp.zeros((2, LANES), f32)
        rows = jnp.concatenate(in_three(top) + in_three(total) + [zero], axis=0)
        stats.append(rows)
    out = 0.0
    for k in range(n):
        y = at_ref[0] ^ k
        block = found_ref[:, y].reshape(slots, width)
        out = out + jnp.dot(jnp.concatenate(weights[k], axis=0), block, preferred_element_type=f32)
    out = out.astype(bf16)
    for c in range(cores):
        for z in range(nz):
            at = c * LANES + z * per
            for j in range(width // LANES):
                outs[z][c, j * per : (j + 1) * per] = out[at : at + per, j * LANES : (j + 1) * LANES]
            outs[z][c, width // LANES * per :] = stats[c].astype(bf16)


def last_kernel(*refs):
    gots, outs = refs[:-2], refs[-2:]
    cores, (per, width) = len(outs), outs[0].shape
    n = len(gots)
    end = width // LANES * per
    both = [gots[k][c, end:].astype(f32) for c in range(cores) for k in range(n)]
    both = both + [jnp.zeros((LANES - 8 * len(both), LANES), f32)]
    both = jnp.concatenate(both, axis=0).T
    for c in range(cores):
        tops, totals = [], []
        for k in range(n):
            i, cols = 8 * (c * n + k), both[k * per : (k + 1) * per]
            tops.append(cols[:, i : i + 1] + cols[:, i + 1 : i + 2] + cols[:, i + 2 : i + 3])
            totals.append(cols[:, i + 3 : i + 4] + cols[:, i + 4 : i + 5] + cols[:, i + 5 : i + 6])
        top = functools.reduce(jnp.maximum, tops)
        shares = [d * jnp.exp(t - top) for t, d in zip(tops, totals)]
        scale = 1.0 / functools.reduce(jnp.add, shares)
        shares = [v * scale for v in shares]
        for j in range(width // LANES):
            out = 0.0
            for k in range(n):
                out = out + gots[k][c, j * per : (j + 1) * per].astype(f32) * shares[k]
            outs[c][:, j * LANES : (j + 1) * LANES] = out.astype(bf16)


def join_kernel(at_ref, keep_ref, got_ref, out_ref):
    out_ref[at_ref[2]] = keep_ref[...]
    out_ref[1 - at_ref[2]] = got_ref[1 - at_ref[2]]


def call(kernel, outs, *args, scalar=False, scratch=(), far=0, mib=16):
    kind = pltpu.MemorySpace.VMEM
    specs = [pl.BlockSpec(memory_space=kind) for _ in args]
    for k in range(far):
        specs[-1 - k] = pl.BlockSpec(memory_space=pl.ANY)
    if scalar:
        specs[0] = pl.BlockSpec(memory_space=pltpu.MemorySpace.SMEM)
    return pl.pallas_call(
        kernel,
        out_shape=outs,
        in_specs=specs,
        out_specs=jax.tree.map(lambda _: pl.BlockSpec(memory_space=kind), outs),
        scratch_shapes=scratch,
        compiler_params=pltpu.CompilerParams(vmem_limit_bytes=mib << 20),
    )(*args)


def shape(*lengths, kind=bf16):
    return jax.ShapeDtypeStruct(lengths, kind)


def shards(tokens, router, w_in, w_out):
    slots = router.shape[1]
    width = tokens.shape[2]
    each = tokens.shape[1]
    nx, nzla, nzlb, nc, nzh, ny = (lax.axis_size(a) for a in AXES)
    assert each == nzh * LANES and slots == nx * nzla * SLOTS
    assert nzh == ny == nx
    here = jnp.stack([lax.axis_index(a).astype(jnp.int32) for a in ("y", "zh", "c")])
    per = LANES // nzh

    own = swap(tokens, "c")

    send, logits = call(
        score_kernel,
        (shape(nx * nzla * nzlb, SLOTS, width + LANES), shape(nc * each, slots, kind=f32)),
        own,
        router,
    )

    arrived = swap(send, ("x", "zla", "zlb"))

    pair = [(0, 1), (1, 0)]
    w_in2 = lax.ppermute(w_in, "c", pair)
    w_out2 = lax.ppermute(w_out, "c", pair)

    block = nc * (slots + 8)
    rows = call(
        row_kernel,
        (shape(block, LANES),) * ny,
        here,
        logits,
        scalar=True,
        scratch=(pltpu.VMEM((ny, block, LANES), bf16),),
    )

    rows = list(rows)
    for k in range(1, ny):
        rows[k] = lax.ppermute(rows[k], "y", [(i, i ^ k) for i in range(ny)])

    out = call(
        ffn_kernel,
        shape(nzla * nzlb, SLOTS, width),
        arrived,
        w_in,
        w_out,
        w_in2,
        w_out2,
        far=2,
        scratch=(
            pltpu.VMEM(w_in.shape, bf16),
            pltpu.VMEM(w_out.shape, bf16),
            pltpu.SemaphoreType.DMA((2,)),
        ),
    )

    got = swap(out, ("zla", "zlb"))

    got = call(pair_kernel, shape(nx * ny, nzla * SLOTS, width), got)

    got, *rows = lax.optimization_barrier((got, *rows))

    found = swap(got, ("x", "y")).reshape(nx, ny, nzla * SLOTS, width)

    block = width // LANES * per + 8
    outs = list(call(mix_kernel, (shape(nc, block, LANES),) * nzh, here, *rows, found, scalar=True))

    for k in range(1, nzh):
        outs[k] = lax.ppermute(outs[k], "zh", [(i, i ^ k) for i in range(nzh)])

    keep, give = call(last_kernel, (shape(per, width),) * nc, *outs)

    got = lax.all_gather(give, "c")

    return call(join_kernel, shape(nc, per, width), here, keep, got, scalar=True)


def solution(mesh):
    torus = Mesh(mesh.devices.reshape(4, 2, 2, 2, 4, 4), AXES)
    placed = (P(None, SEQ, None), P(None, EXP), P(EXP + SEQ, None, None), P(EXP + SEQ, None, None))
    return jax.shard_map(
        shards, mesh=torus, in_specs=placed, out_specs=P(None, SEQ + EXP, None), check_vma=False
    )
```

```python
import functools

import jax
import jax.numpy as jnp
from jax import lax
from jax.experimental import pallas as pl
from jax.experimental.pallas import tpu as pltpu
from jax.sharding import Mesh
from jax.sharding import PartitionSpec as P

SLOTS = 16
LANES = 128
AXES = ("x", "zla", "zlb", "c", "zh", "y")
SEQ = ("x", "zla", "zlb", "c")
EXP = ("zh", "y")
f32, bf16 = jnp.float32, jnp.bfloat16


def swap(tiles, axis):
    return lax.all_to_all(tiles, axis, split_axis=0, concat_axis=0, tiled=True)


def in_three(v):
    hi = v.astype(bf16).astype(f32)
    mid = (v - hi).astype(bf16).astype(f32)
    return [hi, mid, v - hi - mid]


def as_columns(parts):
    lane = lax.broadcasted_iota(jnp.int32, (parts[0].shape[0], LANES), 1)
    out = jnp.zeros(lane.shape, f32)
    for k, part in enumerate(parts):
        out = jnp.where(lane == k, part, out)
    return out.astype(bf16)


def blend(ref, pieces):
    width = ref.shape[-1] - LANES
    tops, totals = [], []
    for k in pieces:
        cols = ref[(*k, slice(None), slice(width, width + LANES))].astype(f32)
        tops.append(cols[:, 0:1] + cols[:, 1:2] + cols[:, 2:3])
        totals.append(cols[:, 3:4] + cols[:, 4:5] + cols[:, 5:6])
    top = functools.reduce(jnp.maximum, tops)
    shares = [s * jnp.exp(t - top) for t, s in zip(tops, totals)]
    scale = 1.0 / functools.reduce(jnp.add, shares)
    out = 0.0
    for k, share in zip(pieces, shares):
        out = out + ref[(*k, slice(None), slice(0, width))].astype(f32) * (share * scale)
    return out


def score_kernel(tok_ref, router_ref, send_ref, logit_ref):
    tok = tok_ref[...].reshape(-1, tok_ref.shape[-1])
    width = tok.shape[1]
    logits = jnp.dot(tok, router_ref[...], preferred_element_type=f32)
    logit_ref[...] = logits
    logits = logits.T
    top = logits.max(axis=1, keepdims=True)
    e1 = jnp.exp(logits - top)
    total = e1.sum(axis=1, keepdims=True)
    part = jnp.dot(e1.astype(bf16), tok, preferred_element_type=f32) * (1.0 / total)
    part = part.astype(bf16)
    stats = as_columns(in_three(top) + in_three(total))
    experts = logits.shape[0] // SLOTS
    copies = send_ref.shape[0] // experts
    for e in range(experts):
        for k in range(copies):
            send_ref[e * copies + k, :, 0:width] = part[e * SLOTS : (e + 1) * SLOTS]
            send_ref[e * copies + k, :, width:] = stats[e * SLOTS : (e + 1) * SLOTS]


def row_kernel(at_ref, logit_ref, *refs):
    outs, hold = refs[:-1], refs[-1]
    n, slots = len(outs), logit_ref.shape[1]
    cores = logit_ref.shape[0] // (n * LANES)
    per = LANES // n
    zero = jnp.zeros((1, LANES), f32)
    for y in range(n):
        rows = []
        for c in range(cores):
            at = [((at_ref[2] ^ c) * n + (at_ref[1] ^ j)) * LANES + y * per for j in range(n)]
            at = [pl.multiple_of(i, per) for i in at]
            logits = jnp.concatenate([logit_ref[pl.ds(i, per)] for i in at], axis=0).T
            top = logits.max(axis=0, keepdims=True)
            hold[y, c * slots : (c + 1) * slots] = jnp.exp(logits - top).astype(bf16)
            rows += in_three(top) + [zero] * 5
        hold[y, cores * slots :] = jnp.concatenate(rows, axis=0).astype(bf16)
    for k in range(n):
        outs[k][...] = hold[at_ref[0] ^ k]


def ffn_kernel(got_ref, a_ref, b_ref, a2_hbm, b2_hbm, out_ref, a2_ref, b2_ref, sem):
    copies = (
        pltpu.make_async_copy(a2_hbm, a2_ref, sem.at[0]),
        pltpu.make_async_copy(b2_hbm, b2_ref, sem.at[1]),
    )
    for copy in copies:
        copy.start()
    rows = blend(got_ref, [(k,) for k in range(got_ref.shape[0])]).astype(bf16)

    def first(a):
        hidden = jnp.dot(rows, a[0], preferred_element_type=f32)
        return jax.nn.gelu(hidden, approximate=True).astype(bf16)

    out = jnp.dot(first(a_ref), b_ref[0], preferred_element_type=f32)
    copies[0].wait()
    hidden = first(a2_ref)
    copies[1].wait()
    out = (out + jnp.dot(hidden, b2_ref[0], preferred_element_type=f32)).astype(bf16)
    for k in range(out_ref.shape[0]):
        out_ref[k] = out


def pair_kernel(got_ref, out_ref):
    pairs = out_ref.shape[1] // SLOTS
    each = got_ref.shape[0] // pairs
    for p in range(pairs):
        out = 0.0
        for k in range(each):
            out = out + got_ref[p * each + k].astype(f32)
        out = out.astype(bf16)
        for k in range(out_ref.shape[0]):
            out_ref[k, p * SLOTS : (p + 1) * SLOTS] = out


def mix_kernel(at_ref, r0, r1, r2, r3, found_ref, *outs):
    rs = (r0, r1, r2, r3)
    n, slots = len(rs), found_ref.shape[0] * found_ref.shape[2]
    width = found_ref.shape[-1]
    cores = r0.shape[0] // slots
    nz = len(outs)
    per = LANES // nz
    weights, stats = [[] for _ in rs], []
    for c in range(cores):
        tops = []
        for r in rs:
            m = r[cores * slots :].astype(f32)[8 * c : 8 * c + 8]
            tops.append(m[0:1] + m[1:2] + m[2:3])
        top = functools.reduce(jnp.maximum, tops)
        e2 = [
            r[c * slots : (c + 1) * slots].astype(f32) * jnp.exp(t - top)
            for r, t in zip(rs, tops)
        ]
        total = functools.reduce(jnp.add, [e.sum(axis=0, keepdims=True) for e in e2])
        scale = 1.0 / total
        for k in range(n):
            weights[k].append((e2[k] * scale).T.astype(bf16))
        zero = jnp.zeros((2, LANES), f32)
        rows = jnp.concatenate(in_three(top) + in_three(total) + [zero], axis=0)
        stats.append(rows)
    out = 0.0
    for k in range(n):
        y = at_ref[0] ^ k
        block = found_ref[:, y].reshape(slots, width)
        out = out + jnp.dot(jnp.concatenate(weights[k], axis=0), block, preferred_element_type=f32)
    out = out.astype(bf16)
    for c in range(cores):
        for z in range(nz):
            at = c * LANES + z * per
            for j in range(width // LANES):
                outs[z][c, j * per : (j + 1) * per] = out[at : at + per, j * LANES : (j + 1) * LANES]
            outs[z][c, width // LANES * per :] = stats[c].astype(bf16)


def last_kernel(*refs):
    gots, outs = refs[:-2], refs[-2:]
    cores, (per, width) = len(outs), outs[0].shape
    n = len(gots)
    end = width // LANES * per
    both = [gots[k][c, end:].astype(f32) for c in range(cores) for k in range(n)]
    both = both + [jnp.zeros((LANES - 8 * len(both), LANES), f32)]
    both = jnp.concatenate(both, axis=0).T
    for c in range(cores):
        tops, totals = [], []
        for k in range(n):
            i, cols = 8 * (c * n + k), both[k * per : (k + 1) * per]
            tops.append(cols[:, i : i + 1] + cols[:, i + 1 : i + 2] + cols[:, i + 2 : i + 3])
            totals.append(cols[:, i + 3 : i + 4] + cols[:, i + 4 : i + 5] + cols[:, i + 5 : i + 6])
        top = functools.reduce(jnp.maximum, tops)
        shares = [d * jnp.exp(t - top) for t, d in zip(tops, totals)]
        scale = 1.0 / functools.reduce(jnp.add, shares)
        shares = [v * scale for v in shares]
        for j in range(width // LANES):
            out = 0.0
            for k in range(n):
                out = out + gots[k][c, j * per : (j + 1) * per].astype(f32) * shares[k]
            outs[c][:, j * LANES : (j + 1) * LANES] = out.astype(bf16)


def join_kernel(at_ref, keep_ref, got_ref, out_ref):
    out_ref[at_ref[2]] = keep_ref[...]
    out_ref[1 - at_ref[2]] = got_ref[1 - at_ref[2]]


def call(kernel, outs, *args, scalar=False, scratch=(), far=0, mib=16):
    kind = pltpu.MemorySpace.VMEM
    specs = [pl.BlockSpec(memory_space=kind) for _ in args]
    for k in range(far):
        specs[-1 - k] = pl.BlockSpec(memory_space=pl.ANY)
    if scalar:
        specs[0] = pl.BlockSpec(memory_space=pltpu.MemorySpace.SMEM)
    return pl.pallas_call(
        kernel,
        out_shape=outs,
        in_specs=specs,
        out_specs=jax.tree.map(lambda _: pl.BlockSpec(memory_space=kind), outs),
        scratch_shapes=scratch,
        compiler_params=pltpu.CompilerParams(vmem_limit_bytes=mib << 20),
    )(*args)


def shape(*lengths, kind=bf16):
    return jax.ShapeDtypeStruct(lengths, kind)


def shards(tokens, router, w_in, w_out):
    slots = router.shape[1]
    width = tokens.shape[2]
    each = tokens.shape[1]
    nx, nzla, nzlb, nc, nzh, ny = (lax.axis_size(a) for a in AXES)
    assert each == nzh * LANES and slots == nx * nzla * SLOTS
    assert nzh == ny == nx
    here = jnp.stack([lax.axis_index(a).astype(jnp.int32) for a in ("y", "zh", "c")])
    per = LANES // nzh

    own = swap(tokens, "c")

    send, logits = call(
        score_kernel,
        (shape(nx * nzla * nzlb, SLOTS, width + LANES), shape(nc * each, slots, kind=f32)),
        own,
        router,
    )

    arrived = swap(send, ("x", "zla", "zlb"))

    pair = [(0, 1), (1, 0)]
    w_in2 = lax.ppermute(w_in, "c", pair)
    w_out2 = lax.ppermute(w_out, "c", pair)

    block = nc * (slots + 8)
    rows = call(
        row_kernel,
        (shape(block, LANES),) * ny,
        here,
        logits,
        scalar=True,
        scratch=(pltpu.VMEM((ny, block, LANES), bf16),),
    )

    rows = list(rows)
    for k in range(1, ny):
        rows[k] = lax.ppermute(rows[k], "y", [(i, i ^ k) for i in range(ny)])

    out = call(
        ffn_kernel,
        shape(nzla * nzlb, SLOTS, width),
        arrived,
        w_in,
        w_out,
        w_in2,
        w_out2,
        far=2,
        scratch=(
            pltpu.VMEM(w_in.shape, bf16),
            pltpu.VMEM(w_out.shape, bf16),
            pltpu.SemaphoreType.DMA((2,)),
        ),
    )

    got = swap(out, ("zla", "zlb"))

    got = call(pair_kernel, shape(nx * ny, nzla * SLOTS, width), got)

    got, *rows = lax.optimization_barrier((got, *rows))

    found = swap(got, ("x", "y")).reshape(nx, ny, nzla * SLOTS, width)

    block = width // LANES * per + 8
    outs = list(call(mix_kernel, (shape(nc, block, LANES),) * nzh, here, *rows, found, scalar=True))

    for k in range(1, nzh):
        outs[k] = lax.ppermute(outs[k], "zh", [(i, i ^ k) for i in range(nzh)])

    keep, give = call(last_kernel, (shape(per, width),) * nc, *outs)

    got = lax.all_gather(give, "c")

    return call(join_kernel, shape(nc, per, width), here, keep, got, scalar=True)


def solution(mesh):
    torus = Mesh(mesh.devices.reshape(4, 2, 2, 2, 4, 4), AXES)
    placed = (P(None, SEQ, None), P(None, EXP), P(EXP + SEQ, None, None), P(EXP + SEQ, None, None))
    return jax.shard_map(
        shards, mesh=torus, in_specs=placed, out_specs=P(None, SEQ + EXP, None), check_vma=False
    )
```

```python
import functools

import jax
import jax.numpy as jnp
from jax import lax
from jax.experimental import pallas as pl
from jax.experimental.pallas import tpu as pltpu
from jax.sharding import Mesh
from jax.sharding import PartitionSpec as P

SLOTS = 16
LANES = 128
AXES = ("x", "zla", "zlb", "c", "zh", "y")
SEQ = ("x", "zla", "zlb", "c")
EXP = ("zh", "y")
f32, bf16 = jnp.float32, jnp.bfloat16


def swap(tiles, axis):
    return lax.all_to_all(tiles, axis, split_axis=0, concat_axis=0, tiled=True)


def in_three(v):
    hi = v.astype(bf16).astype(f32)
    mid = (v - hi).astype(bf16).astype(f32)
    return [hi, mid, v - hi - mid]


def as_columns(parts):
    lane = lax.broadcasted_iota(jnp.int32, (parts[0].shape[0], LANES), 1)
    out = jnp.zeros(lane.shape, f32)
    for k, part in enumerate(parts):
        out = jnp.where(lane == k, part, out)
    return out.astype(bf16)


def blend(ref, pieces):
    width = ref.shape[-1] - LANES
    tops, totals = [], []
    for k in pieces:
        cols = ref[(*k, slice(None), slice(width, width + LANES))].astype(f32)
        tops.append(cols[:, 0:1] + cols[:, 1:2] + cols[:, 2:3])
        totals.append(cols[:, 3:4] + cols[:, 4:5] + cols[:, 5:6])
    top = functools.reduce(jnp.maximum, tops)
    shares = [s * jnp.exp(t - top) for t, s in zip(tops, totals)]
    scale = 1.0 / functools.reduce(jnp.add, shares)
    out = 0.0
    for k, share in zip(pieces, shares):
        out = out + ref[(*k, slice(None), slice(0, width))].astype(f32) * (share * scale)
    return out


def score_kernel(tok_ref, router_ref, send_ref, logit_ref):
    tok = tok_ref[...].reshape(-1, tok_ref.shape[-1])
    width = tok.shape[1]
    logits = jnp.dot(tok, router_ref[...], preferred_element_type=f32)
    logit_ref[...] = logits
    logits = logits.T
    top = logits.max(axis=1, keepdims=True)
    e1 = jnp.exp(logits - top)
    total = e1.sum(axis=1, keepdims=True)
    part = jnp.dot(e1.astype(bf16), tok, preferred_element_type=f32) * (1.0 / total)
    part = part.astype(bf16)
    stats = as_columns(in_three(top) + in_three(total))
    experts = logits.shape[0] // SLOTS
    copies = send_ref.shape[0] // experts
    for e in range(experts):
        for k in range(copies):
            send_ref[e * copies + k, :, 0:width] = part[e * SLOTS : (e + 1) * SLOTS]
            send_ref[e * copies + k, :, width:] = stats[e * SLOTS : (e + 1) * SLOTS]


def row_kernel(at_ref, logit_ref, *refs):
    outs, hold = refs[:-1], refs[-1]
    n, slots = len(outs), logit_ref.shape[1]
    cores = logit_ref.shape[0] // (n * LANES)
    per = LANES // n
    zero = jnp.zeros((1, LANES), f32)
    for y in range(n):
        rows = []
        for c in range(cores):
            at = [((at_ref[2] ^ c) * n + (at_ref[1] ^ j)) * LANES + y * per for j in range(n)]
            at = [pl.multiple_of(i, per) for i in at]
            logits = jnp.concatenate([logit_ref[pl.ds(i, per)] for i in at], axis=0).T
            top = logits.max(axis=0, keepdims=True)
            hold[y, c * slots : (c + 1) * slots] = jnp.exp(logits - top).astype(bf16)
            rows += in_three(top) + [zero] * 5
        hold[y, cores * slots :] = jnp.concatenate(rows, axis=0).astype(bf16)
    for k in range(n):
        outs[k][...] = hold[at_ref[0] ^ k]


def ffn_kernel(got_ref, a_ref, b_ref, a2_hbm, b2_hbm, out_ref, a2_ref, b2_ref, sem):
    copies = (
        pltpu.make_async_copy(a2_hbm, a2_ref, sem.at[0]),
        pltpu.make_async_copy(b2_hbm, b2_ref, sem.at[1]),
    )
    for copy in copies:
        copy.start()
    rows = blend(got_ref, [(k,) for k in range(got_ref.shape[0])]).astype(bf16)

    def part(a, b):
        hidden = jnp.dot(rows, a[0], preferred_element_type=f32)
        hidden = jax.nn.gelu(hidden, approximate=True).astype(bf16)
        return jnp.dot(hidden, b[0], preferred_element_type=f32)

    out = part(a_ref, b_ref)
    for copy in copies:
        copy.wait()
    out = (out + part(a2_ref, b2_ref)).astype(bf16)
    for k in range(out_ref.shape[0]):
        out_ref[k] = out


def pair_kernel(got_ref, out_ref):
    pairs = out_ref.shape[1] // SLOTS
    each = got_ref.shape[0] // pairs
    for p in range(pairs):
        out = 0.0
        for k in range(each):
            out = out + got_ref[p * each + k].astype(f32)
        out = out.astype(bf16)
        for k in range(out_ref.shape[0]):
            out_ref[k, p * SLOTS : (p + 1) * SLOTS] = out


def mix_kernel(at_ref, r0, r1, r2, r3, found_ref, *outs):
    rs = (r0, r1, r2, r3)
    n, slots = len(rs), found_ref.shape[0] * found_ref.shape[2]
    width = found_ref.shape[-1]
    cores = r0.shape[0] // slots
    nz = len(outs)
    per = LANES // nz
    weights, stats = [[] for _ in rs], []
    for c in range(cores):
        tops = []
        for r in rs:
            m = r[cores * slots :].astype(f32)[8 * c : 8 * c + 8]
            tops.append(m[0:1] + m[1:2] + m[2:3])
        top = functools.reduce(jnp.maximum, tops)
        e2 = [
            r[c * slots : (c + 1) * slots].astype(f32) * jnp.exp(t - top)
            for r, t in zip(rs, tops)
        ]
        total = functools.reduce(jnp.add, [e.sum(axis=0, keepdims=True) for e in e2])
        scale = 1.0 / total
        for k in range(n):
            weights[k].append((e2[k] * scale).T.astype(bf16))
        zero = jnp.zeros((2, LANES), f32)
        rows = jnp.concatenate(in_three(top) + in_three(total) + [zero], axis=0)
        stats.append(rows)
    out = 0.0
    for k in range(0, n, 2):
        both = [found_ref[:, at_ref[0] ^ i].reshape(slots, width) for i in (k, k + 1)]
        left = [jnp.concatenate(weights[i], axis=0) for i in (k, k + 1)]
        out = out + jnp.dot(
            jnp.concatenate(left, axis=1),
            jnp.concatenate(both, axis=0),
            preferred_element_type=f32,
        )
    out = out.astype(bf16)
    for c in range(cores):
        for z in range(nz):
            at = c * LANES + z * per
            for j in range(width // LANES):
                outs[z][c, j * per : (j + 1) * per] = out[at : at + per, j * LANES : (j + 1) * LANES]
            outs[z][c, width // LANES * per :] = stats[c].astype(bf16)


def last_kernel(*refs):
    gots, outs = refs[:-2], refs[-2:]
    cores, (per, width) = len(outs), outs[0].shape
    n = len(gots)
    end = width // LANES * per
    both = [gots[k][c, end:].astype(f32) for c in range(cores) for k in range(n)]
    both = both + [jnp.zeros((LANES - 8 * len(both), LANES), f32)]
    both = jnp.concatenate(both, axis=0).T
    for c in range(cores):
        tops, totals = [], []
        for k in range(n):
            i, cols = 8 * (c * n + k), both[k * per : (k + 1) * per]
            tops.append(cols[:, i : i + 1] + cols[:, i + 1 : i + 2] + cols[:, i + 2 : i + 3])
            totals.append(cols[:, i + 3 : i + 4] + cols[:, i + 4 : i + 5] + cols[:, i + 5 : i + 6])
        top = functools.reduce(jnp.maximum, tops)
        shares = [d * jnp.exp(t - top) for t, d in zip(tops, totals)]
        scale = 1.0 / functools.reduce(jnp.add, shares)
        shares = [v * scale for v in shares]
        for j in range(width // LANES):
            out = 0.0
            for k in range(n):
                out = out + gots[k][c, j * per : (j + 1) * per].astype(f32) * shares[k]
            outs[c][:, j * LANES : (j + 1) * LANES] = out.astype(bf16)


def join_kernel(at_ref, keep_ref, got_ref, out_ref):
    out_ref[at_ref[2]] = keep_ref[...]
    out_ref[1 - at_ref[2]] = got_ref[1 - at_ref[2]]


def call(kernel, outs, *args, scalar=False, scratch=(), far=0, mib=16):
    kind = pltpu.MemorySpace.VMEM
    specs = [pl.BlockSpec(memory_space=kind) for _ in args]
    for k in range(far):
        specs[-1 - k] = pl.BlockSpec(memory_space=pl.ANY)
    if scalar:
        specs[0] = pl.BlockSpec(memory_space=pltpu.MemorySpace.SMEM)
    return pl.pallas_call(
        kernel,
        out_shape=outs,
        in_specs=specs,
        out_specs=jax.tree.map(lambda _: pl.BlockSpec(memory_space=kind), outs),
        scratch_shapes=scratch,
        compiler_params=pltpu.CompilerParams(vmem_limit_bytes=mib << 20),
    )(*args)


def shape(*lengths, kind=bf16):
    return jax.ShapeDtypeStruct(lengths, kind)


def shards(tokens, router, w_in, w_out):
    slots = router.shape[1]
    width = tokens.shape[2]
    each = tokens.shape[1]
    nx, nzla, nzlb, nc, nzh, ny = (lax.axis_size(a) for a in AXES)
    assert each == nzh * LANES and slots == nx * nzla * SLOTS
    assert nzh == ny == nx
    here = jnp.stack([lax.axis_index(a).astype(jnp.int32) for a in ("y", "zh", "c")])
    per = LANES // nzh

    own = swap(tokens, "c")

    send, logits = call(
        score_kernel,
        (shape(nx * nzla * nzlb, SLOTS, width + LANES), shape(nc * each, slots, kind=f32)),
        own,
        router,
    )

    arrived = swap(send, ("x", "zla", "zlb"))

    pair = [(0, 1), (1, 0)]
    w_in2 = lax.ppermute(w_in, "c", pair)
    w_out2 = lax.ppermute(w_out, "c", pair)

    block = nc * (slots + 8)
    rows = call(
        row_kernel,
        (shape(block, LANES),) * ny,
        here,
        logits,
        scalar=True,
        scratch=(pltpu.VMEM((ny, block, LANES), bf16),),
    )

    rows = list(rows)
    for k in range(1, ny):
        rows[k] = lax.ppermute(rows[k], "y", [(i, i ^ k) for i in range(ny)])

    out = call(
        ffn_kernel,
        shape(nzla * nzlb, SLOTS, width),
        arrived,
        w_in,
        w_out,
        w_in2,
        w_out2,
        far=2,
        scratch=(
            pltpu.VMEM(w_in.shape, bf16),
            pltpu.VMEM(w_out.shape, bf16),
            pltpu.SemaphoreType.DMA((2,)),
        ),
    )

    got = swap(out, ("zla", "zlb"))

    got = call(pair_kernel, shape(nx * ny, nzla * SLOTS, width), got)

    got, *rows = lax.optimization_barrier((got, *rows))

    found = swap(got, ("x", "y")).reshape(nx, ny, nzla * SLOTS, width)

    block = width // LANES * per + 8
    outs = list(call(mix_kernel, (shape(nc, block, LANES),) * nzh, here, *rows, found, scalar=True))

    for k in range(1, nzh):
        outs[k] = lax.ppermute(outs[k], "zh", [(i, i ^ k) for i in range(nzh)])

    keep, give = call(last_kernel, (shape(per, width),) * nc, *outs)

    got = lax.all_gather(give, "c")

    return call(join_kernel, shape(nc, per, width), here, keep, got, scalar=True)


def solution(mesh):
    torus = Mesh(mesh.devices.reshape(4, 2, 2, 2, 4, 4), AXES)
    placed = (P(None, SEQ, None), P(None, EXP), P(EXP + SEQ, None, None), P(EXP + SEQ, None, None))
    return jax.shard_map(
        shards, mesh=torus, in_specs=placed, out_specs=P(None, SEQ + EXP, None), check_vma=False
    )
```
